32 devices in a mesh: groups: 2 (over y), mom: 4 (over z), tm: 2 (over x), spin: 2 (over core).
Axes of the slice: x: 2, y: 2, z: 4, core: 2. Of those that a mesh axis runs over, the one named last changes fastest.
Arguments:
- fields: bfloat16 [32, 2, 2, 2, 256, 256], P(('groups', 'mom'), 'tm', 'spin'), parts along dimension 0, may hold values from -1.5 to 1.5
- pair_slot: int32 [2, 4, 4, 3], replicated, may hold values from 0 to 3, as said below
- channel: int32 [2, 4, 4, 3], replicated, may hold values from 0 to 3
- cg_index: int32 [2, 4, 4, 3], replicated, may hold values from 0 to 63
- cg_table: float32 [64], replicated, may hold values from -0.6 to 0.6
Outputs:
- operators: bfloat16 [4, 4, 2, 2, 256, 256], P(None, ('groups', 'tm'), 'spin', None, 'mom'), parts along dimension 1
The draws below stay inside these ranges and needn't reach their ends.
There are 2 independent parts, one for each index of `groups`. The reference program is written for one: setup_inputs(seed, part) draws one part's arguments, and reference() takes and returns one part's arrays. A program takes and returns all parts, laid end to end along the dimension named above; an argument that names none is the same for every part. Nothing has to cross between parts.
Inputs may be any that keep to these rules, and one draw needn't show every extreme that they name: For every round and every index of mom, the 4 x 3 entries of pair_slot take exactly 2 distinct values.
All inputs are finite; a program needn't handle non-finite values.
Results may differ from the reference program's by a relative error of at most 0.0012.
Values may be sent and summed in bfloat16 or wider, within the bound.
No kernel may reach another device: no remote copies, remote signals or barrier semaphores. Data moves between devices by JAX's collectives and lax.ppermute only.
A program may use at most 64 MiB of HBM per device.

```python
import jax
import jax.numpy as jnp
from jax import lax

MODES = 256
MOM_DEV = 4
ROUNDS = 2
PAIRS = 3
CHANNELS = 4
NCG = 64
MOMENTA = 16
TSLICES = 2
GAMMAS = 2
N_MOM = 4


def draw_pair_slot(key, part):
    row_count = ROUNDS * N_MOM
    row_keys = jax.random.split(key, row_count)

    def one_row(row_key):
        key_choose, key_picks, key_shuffle = jax.random.split(row_key, 3)
        chosen = jax.random.permutation(key_choose, MOM_DEV)[:MOM_DEV // 2]
        pick_list = jax.random.randint(key_picks, (MOM_DEV * PAIRS,), 0, MOM_DEV // 2)
        pick_list = pick_list.at[:MOM_DEV // 2].set(jnp.arange(MOM_DEV // 2, dtype=jnp.int32))
        entries = chosen[pick_list]
        entries = jax.random.permutation(key_shuffle, entries)
        return entries.reshape(MOM_DEV, PAIRS)
    table_rows = jax.vmap(one_row)(row_keys)
    return table_rows.reshape(ROUNDS, N_MOM, MOM_DEV, PAIRS).astype(jnp.int32)


def set_ends(values, rng, low, top_value):
    index_at = [jax.random.randint(jax.random.fold_in(rng, axis), (), 0, length) for axis, length in enumerate(values.shape)]
    widest = values.shape.index(max(values.shape))
    beside = index_at[:widest] + [(index_at[widest] + 1) % values.shape[widest]] + index_at[widest + 1:]
    return values.at[tuple(index_at)].set(low).at[tuple(beside)].set(top_value)


def levels(own_key, dims, shards, smallest, largest):
    level = 1.0
    for position, shards_of in shards:
        draws = jax.random.uniform(jax.random.fold_in(jax.random.fold_in(own_key, 6), position), (shards_of,), jnp.float32, smallest / len(shards), largest / len(shards))
        level = level * jnp.repeat(jnp.exp(draws), dims[position] // shards_of).reshape((-1,) + (1,) * (len(dims) - 1 - position))
    return level


def bell_draw(stream_key, dims, scale, bound, cuts=(), kind=jnp.bfloat16):
    level = levels(stream_key, dims, cuts, -0.22, 0.18) if cuts else 1.0
    values = jax.random.normal(stream_key, dims, jnp.float32) * scale * level
    return jnp.minimum(jnp.maximum(values, -bound), bound).astype(kind)


def setup_inputs(seed: int = 0, part: int = 0) -> dict:
    seeds = jax.random.split(jax.random.key(seed), 6)
    part_splits = jax.random.split(jax.random.fold_in(seeds[5], part), 6)
    return {
        "fields": bell_draw(part_splits[0], (MOMENTA, TSLICES, GAMMAS, 2, MODES, MODES), 0.25, 1.5, ((0, 4), (1, 2), (2, 2))),
        "pair_slot": draw_pair_slot(jax.random.fold_in(seeds[5], 71), part),
        "channel": set_ends(jax.random.randint(seeds[2], (ROUNDS, N_MOM, MOM_DEV, PAIRS), 0, CHANNELS), jax.random.fold_in(seeds[2], 1), 0, CHANNELS - 1).astype(jnp.int32),
        "cg_index": set_ends(jax.random.randint(seeds[3], (ROUNDS, N_MOM, MOM_DEV, PAIRS), 0, NCG), jax.random.fold_in(seeds[3], 1), 0, NCG - 1).astype(jnp.int32),
        "cg_table": bell_draw(seeds[4], (NCG,), 0.1, 0.6, (), jnp.float32),
    }


def complex_product(left_blocks, right_blocks):
    left_real = left_blocks[:, :, :, 0]
    left_imag = left_blocks[:, :, :, 1]
    right_real = right_blocks[:, :, :, 0]
    right_imag = right_blocks[:, :, :, 1]
    form = "stgxy,stgyz->stgxz"
    real_part = jnp.einsum(form, left_real, right_real) - jnp.einsum(form, left_imag, right_imag)
    imag_part = jnp.einsum(form, left_real, right_imag) + jnp.einsum(form, left_imag, right_real)
    return jnp.stack([real_part, imag_part], axis=3)


def channel_weights(chan_row, index_row, cg_table):
    table_ids = jnp.arange(cg_table.shape[0], dtype=jnp.int32)
    coefficient = jnp.sum(jnp.where(index_row[:, None] == table_ids[None, :], cg_table[None, :], jnp.zeros((), cg_table.dtype)), axis=1)
    chan_ids = jnp.arange(CHANNELS, dtype=jnp.int32)
    return jnp.where(chan_row[None, :] == chan_ids[:, None], coefficient[None, :], jnp.zeros((), cg_table.dtype))


def reference(fields, pair_slot, channel, cg_index, cg_table):
    log_size = N_MOM.bit_length() - 1
    blocks = fields.reshape(N_MOM, MOM_DEV, TSLICES, GAMMAS, 2, MODES, MODES)

    def per_device(accumulated, device_idx):
        own_blocks = lax.dynamic_index_in_dim(blocks, device_idx, 0, keepdims=False).astype(jnp.float32)
        for round_idx in range(ROUNDS):
            shift_bit = (log_size - 1 - round_idx) % log_size
            partner = jnp.bitwise_xor(device_idx, jnp.int32(1 << shift_bit)).astype(jnp.int32)
            remote = lax.dynamic_index_in_dim(blocks, partner, 0, keepdims=False)
            for pair_idx in range(PAIRS):
                slots = pair_slot[round_idx, device_idx, :, pair_idx].astype(jnp.int32)
                right_blocks = jnp.take(remote, slots, axis=0).astype(jnp.float32)
                product = complex_product(own_blocks, right_blocks)
                weights = channel_weights(channel[round_idx, device_idx, :, pair_idx], cg_index[round_idx, device_idx, :, pair_idx], cg_table)
                accumulated = accumulated + jnp.einsum("cs,stgpxz->ctgpxz", weights, product, precision=lax.Precision.HIGHEST)
        return accumulated, None

    start = jnp.zeros((CHANNELS, TSLICES, GAMMAS, 2, MODES, MODES), jnp.float32)
    summed, _ = lax.scan(per_device, start, jnp.arange(N_MOM, dtype=jnp.int32))
    return summed.astype(jnp.bfloat16)
```

```python
import functools

import jax
import jax.numpy as jnp
from jax import lax
from jax.experimental import pallas as pl
from jax.experimental.pallas import tpu as pltpu
from jax.sharding import PartitionSpec as P

ROUNDS = 2
CHANNELS = 4
SLOTS = 2
CHUNKS = 2
LEVELS = 32000.0
SCALE_ROWS = 16
LOWEST, HIGHEST = -110, 31

VMEM = pl.BlockSpec(memory_space=pltpu.VMEM)
SMEM = pl.BlockSpec(memory_space=pltpu.SMEM)


def two_slots(pair_slot, round_idx, index, mom_dev, pair_count):
    entries = [pair_slot[round_idx, index, s, k] for s in range(mom_dev) for k in range(pair_count)]
    return functools.reduce(jnp.minimum, entries), functools.reduce(jnp.maximum, entries)


def exact_power(exponent):
    size = jnp.abs(exponent)
    negative = exponent < 0
    power = jnp.ones(exponent.shape, jnp.float32)
    for bit in range(7):
        step = jnp.where(negative, 2.0 ** -(1 << bit), 2.0 ** (1 << bit))
        power = jnp.where((size >> bit) & 1 == 1, power * step, power)
    return power


def pick_kernel(bits, pair_slot, fields, *outs):
    mom_dev, pair_count = pair_slot.shape[2], pair_slot.shape[3]
    me = lax.axis_index("mom")
    width = outs[0].shape[-1]
    for r, bit in enumerate(bits):
        slots = two_slots(pair_slot, r, me ^ bit, mom_dev, pair_count)
        for d, slot in enumerate(slots):
            block = fields[slot]
            for q in range(CHUNKS):
                outs[q * ROUNDS + r][d] = block[:, :, q * width : (q + 1) * width]


def product_kernel(count, pair_slot, channel, cg_index, cg_table, fields, *refs):
    rights, (own, *sent), (weights, packed) = refs[:ROUNDS], refs[ROUNDS : ROUNDS + count], refs[ROUNDS + count :]
    mom_dev, pair_count = pair_slot.shape[2], pair_slot.shape[3]
    modes, width = fields.shape[2], rights[0].shape[-1]
    rows = modes // count
    me = lax.axis_index("mom")

    for i in range(ROUNDS * SLOTS * mom_dev * CHANNELS):
        weights[i] = jnp.float32(0)
    for r in range(ROUNDS):
        low, _ = two_slots(pair_slot, r, me, mom_dev, pair_count)
        for s in range(mom_dev):
            for k in range(pair_count):
                d = jnp.where(pair_slot[r, me, s, k] == low, 0, 1)
                at = ((r * SLOTS + d) * mom_dev + s) * CHANNELS + channel[r, me, s, k]
                weights[at] = weights[at] + cg_table[cg_index[r, me, s, k]]

    for r in range(ROUNDS):
        for d in range(SLOTS):
            real, imag = rights[r][d, 0], rights[r][d, 1]
            packed[r * SLOTS + d, :modes, :width] = real
            packed[r * SLOTS + d, :modes, width:] = imag
            packed[r * SLOTS + d, modes:, :width] = -imag
            packed[r * SLOTS + d, modes:, width:] = real

    for hop in [*range(1, count), 0]:
        start = pl.multiple_of((me ^ hop) * rows, rows)
        left = jnp.concatenate(
            [
                jnp.concatenate([fields[s, 0, pl.ds(start, rows), :], fields[s, 1, pl.ds(start, rows), :]], axis=1)
                for s in range(mom_dev)
            ],
            axis=0,
        )
        totals = [None] * CHANNELS
        for rd in range(ROUNDS * SLOTS):
            term = jnp.dot(left, packed[rd], preferred_element_type=jnp.float32)
            for s in range(mom_dev):
                part = term[s * rows : (s + 1) * rows]
                for c in range(CHANNELS):
                    weighted = weights[(rd * mom_dev + s) * CHANNELS + c] * part
                    totals[c] = weighted if totals[c] is None else totals[c] + weighted
        if hop == 0:
            for c in range(CHANNELS):
                own[(2 * c) * rows : (2 * c + 1) * rows] = totals[c][:, :width]
                own[(2 * c + 1) * rows : (2 * c + 2) * rows] = totals[c][:, width:]
        else:
            out = sent[hop - 1]
            row_id = lax.broadcasted_iota(jnp.int32, (SCALE_ROWS, width), 0)
            kept = jnp.zeros((SCALE_ROWS, width), jnp.int32)
            for c in range(CHANNELS):
                most = jnp.max(jnp.abs(totals[c]), axis=0, keepdims=True)
                exponent = jnp.ceil(jnp.log2(jnp.maximum(most, 2.0**LOWEST))).astype(jnp.int32)
                exponent = jnp.minimum(jnp.maximum(exponent, LOWEST), HIGHEST)
                coded = jnp.round(totals[c] * (exact_power(-exponent) * LEVELS)).astype(jnp.int32)
                for p in range(2):
                    at = 2 * c + p
                    out[at * rows : (at + 1) * rows] = coded[:, p * width : (p + 1) * width].astype(jnp.int16)
                    kept = jnp.where(row_id == at, exponent[:, p * width : (p + 1) * width], kept)
            out[2 * CHANNELS * rows :] = kept.astype(jnp.int16)


def total_kernel(count, *refs):
    ins, out = refs[:-1], refs[-1]
    rows, width = out.shape[2], ins[0].shape[-1]
    for q in range(CHUNKS):
        own, *came = ins[q * count : (q + 1) * count]
        for hop in came:
            assert hop.shape[1] == width
        scales = [
            exact_power(hop[2 * CHANNELS * rows :].astype(jnp.int32)) * (1.0 / LEVELS) for hop in came
        ]
        for at in range(2 * CHANNELS):
            total = own[at * rows : (at + 1) * rows]
            for hop, scale in zip(came, scales):
                total = total + hop[at * rows : (at + 1) * rows].astype(jnp.float32) * scale[at : at + 1]
            out[at // 2, at % 2, :, q * width : (q + 1) * width] = total.astype(out.dtype)


def per_device(fields, pair_slot, channel, cg_index, cg_table):
    mom_dev, modes = fields.shape[0], fields.shape[-1]
    count = lax.axis_size("mom")
    log_size = count.bit_length() - 1
    bits = [1 << ((log_size - 1 - r) % log_size) for r in range(ROUNDS)]
    rows, width = modes // count, modes // CHUNKS
    blocks = fields.reshape(mom_dev, 2, modes, modes)

    def exchange(x, bit):
        return lax.ppermute(x, "mom", [(i, i ^ bit) for i in range(count)])

    picked = pl.pallas_call(
        functools.partial(pick_kernel, bits),
        out_shape=[jax.ShapeDtypeStruct((SLOTS, 2, modes, width), fields.dtype)] * (CHUNKS * ROUNDS),
        in_specs=[SMEM, VMEM],
        out_specs=[VMEM] * (CHUNKS * ROUNDS),
        name="pick",
    )(pair_slot, blocks)
    rights = [exchange(picked[q * ROUNDS + r], bits[r]) for q in range(CHUNKS) for r in range(ROUNDS)]

    flat = 2 * CHANNELS * rows
    products = pl.pallas_call(
        functools.partial(product_kernel, count),
        out_shape=[jax.ShapeDtypeStruct((flat, width), jnp.float32)]
        + [jax.ShapeDtypeStruct((flat + SCALE_ROWS, width), jnp.int16)] * (count - 1),
        in_specs=[SMEM] * 4 + [VMEM] * (1 + ROUNDS),
        out_specs=[VMEM] * count,
        scratch_shapes=[
            pltpu.SMEM((ROUNDS * SLOTS * mom_dev * CHANNELS,), jnp.float32),
            pltpu.VMEM((ROUNDS * SLOTS, 2 * modes, 2 * width), fields.dtype),
        ],
        cost_estimate=pl.CostEstimate(
            flops=ROUNDS * SLOTS * mom_dev * 8 * modes * modes * width,
            bytes_accessed=4 * modes * modes * mom_dev,
            transcendentals=0,
        ),
        name="products",
    )
    gathered = []
    for q in range(CHUNKS):
        own, *sent = products(
            pair_slot, channel, cg_index, cg_table, blocks, *rights[q * ROUNDS : (q + 1) * ROUNDS]
        )
        gathered += [own] + [exchange(block, hop + 1) for hop, block in enumerate(sent)]

    out = pl.pallas_call(
        functools.partial(total_kernel, count),
        out_shape=jax.ShapeDtypeStruct((CHANNELS, 2, rows, modes), jnp.bfloat16),
        in_specs=[VMEM] * len(gathered),
        out_specs=VMEM,
        name="total",
    )(*gathered)
    return out.reshape(CHANNELS, 1, 1, 2, rows, modes)


def solution(mesh):
    placed = (P(("groups", "mom"), "tm", "spin", None, None, None), P(), P(), P(), P())
    return jax.shard_map(
        per_device,
        mesh=mesh,
        in_specs=placed,
        out_specs=P(None, ("groups", "tm"), "spin", None, "mom", None),
        check_vma=False,
    )
```
